256 devices in a mesh: nodes: 32 (over y, z), feat: 8 (over x, core).
Axes of the slice: x: 4, y: 4, z: 8, core: 2. Of those that a mesh axis runs over, the one named last changes fastest.
Arguments:
- features: bfloat16 [32768, 1024], P('nodes', 'feat'), may hold values from -6 to 6
- ghosts: int32 [1024, 2], P('nodes'), may hold values from 0 to 7, as said below
- slots: int32 [256, 24], P('nodes'), may hold values from 0 to 63
- tile_ids: int32 [256, 24], P('nodes'), may hold values from 0 to 15
- degrees: int32 [256], P('nodes'), may hold values from 1 to 24, 2048 in all
- tile_table: bfloat16 [16, 128, 128], replicated, may hold values from -0.5 to 0.5
- weight_one: bfloat16 [1024, 1024], P(None, 'feat'), may hold values from -0.1875 to 0.1875
- weight_two: bfloat16 [1024, 1024], P(None, 'feat'), may hold values from -0.1875 to 0.1875
- cotangent: bfloat16 [32768, 1024], P('nodes', 'feat'), may hold values from -0.15625 to 0.15625
Outputs:
- output: bfloat16 [32768, 1024], P('nodes', 'feat')
- grad_one: float32 [1024, 1024], P('nodes', 'feat')
- grad_two: float32 [1024, 1024], P('nodes', 'feat')
The draws below stay inside these ranges and needn't reach their ends.
Inputs may be any that keep to these rules, and one draw needn't show every extreme that they name: `ghosts`: row d * 32 + p holds 2 distinct block indices of device p. The degrees sum to 2048; the largest is 24.
All inputs are finite; a program needn't handle non-finite values. No bound on the sum of `degrees` on one device may be relied on, other than what follows from the above.
Results may differ from the reference program's by a relative error of at most 0.0061.
Values may be sent and summed in bfloat16 or wider, within the bound.
A program may use at most 64 MiB of HBM per device.

```python
import math
import jax
import jax.numpy as jnp
import numpy as np
from jax import lax

H = 1024
BS = 128
BLK_DEV = 8
GHOST = 2
KMAX = 24
DEG = 8
NTAB = 16
NB = 256
NODES = 32768
SLOTS = 64
N_NODES = 32


def draw_ghosts(key, part):
    pair_rows = N_NODES * N_NODES
    scores = jax.random.randint(key, (pair_rows, BLK_DEV), 0, 1 << 20) * BLK_DEV
    scores = scores + jnp.arange(BLK_DEV, dtype=jnp.int32)[None, :]
    ranking = jnp.argsort(scores, axis=1, stable=True)
    return ranking[:, :GHOST].astype(jnp.int32)


def place_ends(values, rng, low, largest):
    index_at = [jax.random.randint(jax.random.fold_in(rng, axis), (), 0, length) for axis, length in enumerate(values.shape)]
    widest = values.shape.index(max(values.shape))
    next_to = index_at[:widest] + [(index_at[widest] + 1) % values.shape[widest]] + index_at[widest + 1:]
    return values.at[tuple(index_at)].set(low).at[tuple(next_to)].set(largest)


def level_of(rng, shape, pieces, low, high):
    gain = 1.0
    for dim, shards_of in pieces:
        heights = jax.random.uniform(jax.random.fold_in(jax.random.fold_in(rng, 6), dim), (shards_of,), jnp.float32, low / len(pieces), high / len(pieces))
        gain = gain * jnp.repeat(jnp.exp(heights), shape[dim] // shards_of).reshape((-1,) + (1,) * (len(shape) - 1 - dim))
    return gain


def length_profile(count, total, limit, slope):
    loads = [(1 << 20) // math.isqrt(rank ** slope) + 1 for rank in range(2, count + 1)]
    rest, holding = total - limit - (count - 1), [1] * (count - 1)
    while rest > 0:
        free = [i for i in range(count - 1) if holding[i] < limit]
        mass, remaining = sum([loads[i] for i in free]), rest
        for i in free:
            more = min(limit - holding[i], max(1, remaining * loads[i] // mass), rest)
            holding[i] = holding[i] + more
            rest = rest - more
    return np.array([limit] + holding)


def ragged_sizes(key, amount, total, reach, slope):
    if amount == 2:
        one = jax.random.randint(key, (), max(1, total - reach), min(reach, total - 1) + 1)
        return jnp.stack([one, total - one])
    lengths = jnp.asarray(length_profile(amount, total, reach, slope), jnp.int32)
    twos = (amount - 1) // 2
    giver, sink = lengths[1:1 + 2 * twos:2], lengths[2:2 + 2 * twos:2]
    room = jnp.minimum(giver - 1, reach - sink)
    moved = jax.random.randint(jax.random.fold_in(key, 1), (twos,), 0, 1 << 20) % (room + 1)
    lengths = lengths.at[1:1 + 2 * twos:2].set(giver - moved).at[2:2 + 2 * twos:2].set(sink + moved)
    return lengths[jax.random.permutation(jax.random.fold_in(key, 2), amount)]


def normal_values(key, shape, scale, bound, shards=(), held_as=jnp.bfloat16):
    loudness = level_of(key, shape, shards, -0.22, 0.18) if shards else 1.0
    array = jax.random.normal(key, shape, jnp.float32) * scale * loudness
    return jnp.minimum(jnp.maximum(array, -bound), bound).astype(held_as)


def setup_inputs(seed: int = 0) -> dict:
    keys = jax.random.split(jax.random.key(seed), 10)
    features = normal_values(keys[0], (NODES, H), 1.0, 6.0, ((0, 32), (1, 8)))
    ghosts = draw_ghosts(jax.random.fold_in(keys[9], 71), 0)
    slots = place_ends(jax.random.randint(keys[2], (NB, KMAX), 0, SLOTS), jax.random.fold_in(keys[2], 1), 0, SLOTS - 1).astype(jnp.int32)
    tile_ids = place_ends(jax.random.randint(keys[3], (NB, KMAX), 0, NTAB), jax.random.fold_in(keys[3], 1), 0, NTAB - 1).astype(jnp.int32)
    degrees = ragged_sizes(keys[4], NB, NB * DEG, KMAX, 2).astype(jnp.int32)
    tile_table = normal_values(keys[5], (NTAB, BS, BS), BS ** -0.5, 0.5)
    weight_one = normal_values(keys[6], (H, H), H ** -0.5, 0.1875, ((1, 8),))
    weight_two = normal_values(keys[7], (H, H), H ** -0.5, 0.1875, ((1, 8),))
    cotangent = normal_values(keys[8], (NODES, H), 0.01, 0.15625, ((0, 32), (1, 8)))
    return {"features": features, "ghosts": ghosts, "slots": slots, "tile_ids": tile_ids, "degrees": degrees, "tile_table": tile_table, "weight_one": weight_one, "weight_two": weight_two, "cotangent": cotangent}


def ghost_index(ghosts, slots):
    owner_dev = jnp.arange(NB, dtype=jnp.int32) // BLK_DEV
    peer_dev = slots // GHOST
    column = slots % GHOST
    local_block = ghosts[owner_dev[:, None] * N_NODES + peer_dev, column]
    return (peer_dev * BLK_DEV + local_block).astype(jnp.int32)

def entry_weights(degrees):
    position = jnp.arange(KMAX, dtype=jnp.int32)[None, :]
    inverse_root = lax.rsqrt(degrees.astype(jnp.float32))[:, None]
    return jnp.where(position < degrees[:, None], inverse_root, jnp.zeros_like(inverse_root))

def propagate(values, neighbour, tile_ids, weights, tile_table):
    grouped = values.reshape(NB, BS, values.shape[1])
    tile_rows = tile_table.astype(jnp.float32)

    def one_block(block_args):
        row_nb, row_tiles, row_weights, own_block = block_args
        near_rows = grouped[row_nb]
        picked = tile_rows[row_tiles]
        products = jnp.einsum('kij,kjf->kif', picked, near_rows, precision=lax.Precision.HIGHEST)
        return own_block + jnp.einsum('k,kif->if', row_weights, products, precision=lax.Precision.HIGHEST)
    result = lax.map(one_block, (neighbour, tile_ids, weights, grouped))
    return result.reshape(values.shape)

def back_spread(grad_agg, ghosts, slots, tile_ids, weights, tile_table):
    width = grad_agg.shape[1]
    grouped = grad_agg.astype(jnp.float32).reshape(NB, BS, width)
    tile_rows = tile_table.astype(jnp.float32)
    slot_ids = jnp.arange(SLOTS, dtype=jnp.int32)
    peer_dev = slot_ids // GHOST
    column = slot_ids % GHOST

    def one_device(carry, device):
        first = (device * BLK_DEV).astype(jnp.int32)
        dev_blocks = lax.dynamic_slice_in_dim(grouped, first, BLK_DEV, 0)
        dev_slots = lax.dynamic_slice_in_dim(slots, first, BLK_DEV, 0)
        dev_tiles = lax.dynamic_slice_in_dim(tile_ids, first, BLK_DEV, 0)
        dev_weights = lax.dynamic_slice_in_dim(weights, first, BLK_DEV, 0)

        def one_block(partial_value, block_args):
            row_slots, row_tiles, row_weights, block = block_args
            products = jnp.einsum('kji,jf->kif', tile_rows[row_tiles], block, precision=lax.Precision.HIGHEST)
            scaled = row_weights[:, None, None] * products
            return (partial_value + jax.ops.segment_sum(scaled, row_slots, num_segments=SLOTS), None)
        start_value = jnp.zeros((SLOTS, BS, width), jnp.float32)
        partial_value, unused = lax.scan(one_block, start_value, (dev_slots, dev_tiles, dev_weights, dev_blocks))
        rounded = lax.optimization_barrier(partial_value.astype(jnp.bfloat16)).astype(jnp.float32)
        local_block = ghosts[device * N_NODES + peer_dev, column]
        target = (peer_dev * BLK_DEV + local_block).astype(jnp.int32)
        return (carry.at[target].add(rounded), None)
    total = jnp.zeros((NB, BS, width), jnp.float32)
    total, unused = lax.scan(one_device, total, jnp.arange(N_NODES, dtype=jnp.int32))
    return (grouped + total).reshape(grad_agg.shape)

def reference(features, ghosts, slots, tile_ids, degrees, tile_table, weight_one, weight_two, cotangent):
    neighbour = ghost_index(ghosts, slots)
    weights = entry_weights(degrees)

    def spread(field):
        return propagate(field, neighbour, tile_ids, weights, tile_table)
    agg_one = spread(features.astype(jnp.float32)).astype(jnp.bfloat16)
    pre_one = jnp.dot(agg_one, weight_one, preferred_element_type=jnp.float32)
    hidden = jax.nn.silu(pre_one).astype(jnp.bfloat16)
    agg_two = spread(hidden.astype(jnp.float32)).astype(jnp.bfloat16)
    output = jnp.dot(agg_two, weight_two, preferred_element_type=jnp.float32).astype(jnp.bfloat16)
    grad_two = jnp.dot(agg_two.T, cotangent, preferred_element_type=jnp.float32)
    grad_agg = jnp.dot(cotangent, weight_two.T, preferred_element_type=jnp.float32).astype(jnp.bfloat16)
    back_hidden = back_spread(grad_agg, ghosts, slots, tile_ids, weights, tile_table)
    sigmoid_pre = jax.nn.sigmoid(pre_one)
    back_pre = (back_hidden * sigmoid_pre * (1.0 + pre_one * (1.0 - sigmoid_pre))).astype(jnp.bfloat16)
    grad_one = jnp.dot(agg_one.T, back_pre, preferred_element_type=jnp.float32)
    return (output, grad_one, grad_two)
```

```python
import jax
import jax.numpy as jnp
from jax import lax
from jax.sharding import PartitionSpec as P

entry_step = 8


def entry_weights(degrees, slot_width):
    position = lax.broadcasted_iota(jnp.int32, (degrees.shape[0], slot_width), 1)
    inverse_root = lax.rsqrt(degrees.astype(jnp.float32))[:, None]
    return jnp.where(position < degrees[:, None], inverse_root, 0.0)


def collect(ghost_rows, slots, tile_ids, weights, tile_table, passes):
    block_count = slots.shape[0]
    block_size = ghost_rows.shape[1]
    feat_width = ghost_rows.shape[2]

    def collect_advance(turn_index, running):
        first_entry = turn_index * entry_step
        near_ids = lax.dynamic_slice_in_dim(slots, first_entry, entry_step, 1)
        tile_pick = lax.dynamic_slice_in_dim(tile_ids, first_entry, entry_step, 1)
        entry_share = lax.dynamic_slice_in_dim(weights, first_entry, entry_step, 1)
        near_rows = ghost_rows[near_ids]
        picked = tile_table[tile_pick]
        products = jnp.einsum(
            "bkij,bkjf->bkif", picked, near_rows, preferred_element_type=jnp.float32
        )
        return running + jnp.sum(entry_share[:, :, None, None] * products, axis=1)

    start_value = jnp.zeros((block_count, block_size, feat_width), jnp.float32)
    return lax.fori_loop(0, passes, collect_advance, start_value)


def neighbours(values, requests, slots, tile_ids, weights, tile_table, passes):
    block_count = slots.shape[0]
    block_size = tile_table.shape[1]
    blocks = values.reshape(block_count, block_size, values.shape[1])
    outgoing = blocks[requests]
    arrived = lax.all_to_all(outgoing, "nodes", split_axis=0, concat_axis=0, tiled=True)
    flat_rows = arrived.reshape(-1, block_size, arrived.shape[3])
    running = collect(flat_rows, slots, tile_ids, weights, tile_table, passes)
    return (blocks.astype(jnp.float32) + running).astype(jnp.bfloat16).reshape(values.shape)


def scatter_back(grad_rows, requests, slots, tile_ids, weights, tile_table, passes, peer_count):
    block_count = slots.shape[0]
    block_size = tile_table.shape[1]
    feat_width = grad_rows.shape[1]
    blocks = grad_rows.reshape(block_count, block_size, feat_width)
    slot_total = requests.shape[0] * requests.shape[1]

    def scatter_advance(turn_index, running):
        first_entry = turn_index * entry_step
        near_ids = lax.dynamic_slice_in_dim(slots, first_entry, entry_step, 1)
        tile_pick = lax.dynamic_slice_in_dim(tile_ids, first_entry, entry_step, 1)
        entry_share = lax.dynamic_slice_in_dim(weights, first_entry, entry_step, 1)
        picked = tile_table[tile_pick]
        products = jnp.einsum("bkji,bjf->bkif", picked, blocks, preferred_element_type=jnp.float32)
        scaled = entry_share[:, :, None, None] * products
        return running + jax.ops.segment_sum(
            scaled.reshape(-1, block_size, feat_width),
            near_ids.reshape(-1),
            num_segments=slot_total,
        )

    start_value = jnp.zeros((slot_total, block_size, feat_width), jnp.float32)
    outbound = lax.fori_loop(0, passes, scatter_advance, start_value)
    outgoing = outbound.astype(jnp.bfloat16).reshape(peer_count, -1, block_size, feat_width)
    arrived = lax.all_to_all(outgoing, "nodes", split_axis=0, concat_axis=0, tiled=True)
    flat_rows = arrived.reshape(-1, block_size, arrived.shape[3]).astype(jnp.float32)
    running = jax.ops.segment_sum(flat_rows, requests.reshape(-1), num_segments=block_count)
    return (blocks.astype(jnp.float32) + running).reshape(grad_rows.shape)


def widen(values):
    return lax.all_gather(values, "feat", axis=1, tiled=True)


def weight_grad(wide_rows, local_rows):
    shares = lax.dot_general(
        wide_rows, local_rows, (((0,), (0,)), ((), ())), preferred_element_type=jnp.float32
    )
    peer_count = lax.axis_size("nodes")
    shares = shares.reshape(peer_count, -1, shares.shape[1])
    arrived = lax.all_to_all(shares, "nodes", split_axis=0, concat_axis=0, tiled=True)
    return jnp.sum(arrived, axis=0)


def on_device(
    features, ghosts, slots, tile_ids, degrees, tile_table, weight_one, weight_two, cotangent
):
    peer_count = lax.axis_size("nodes")
    requests = lax.all_to_all(ghosts, "nodes", split_axis=0, concat_axis=0, tiled=True)
    weights = entry_weights(degrees, slots.shape[1])
    passes = slots.shape[1] // entry_step
    agg_one = neighbours(features, requests, slots, tile_ids, weights, tile_table, passes)
    wide_one = widen(agg_one)
    pre_one = jnp.dot(wide_one, weight_one, preferred_element_type=jnp.float32)
    hidden = jax.nn.silu(pre_one).astype(jnp.bfloat16)
    agg_two = neighbours(hidden, requests, slots, tile_ids, weights, tile_table, passes)
    wide_two = widen(agg_two)
    output = jnp.dot(wide_two, weight_two, preferred_element_type=jnp.float32).astype(jnp.bfloat16)
    grad_two = weight_grad(wide_two, cotangent)
    partial_terms = lax.dot_general(
        cotangent, weight_two, (((1,), (1,)), ((), ())), preferred_element_type=jnp.float32
    )
    grad_sum = lax.psum_scatter(partial_terms, "feat", scatter_dimension=1, tiled=True)
    grad_agg = grad_sum.astype(jnp.bfloat16)
    back_hidden = scatter_back(
        grad_agg, requests, slots, tile_ids, weights, tile_table, passes, peer_count
    )
    sigmoid_pre = jax.nn.sigmoid(pre_one)
    back_pre = (back_hidden * sigmoid_pre * (1.0 + pre_one * (1.0 - sigmoid_pre))).astype(
        jnp.bfloat16
    )
    grad_one = weight_grad(wide_one, back_pre)
    return (output, grad_one, grad_two)


def solution(mesh):
    return jax.shard_map(
        on_device,
        mesh=mesh,
        in_specs=(
            P("nodes", "feat"),
            P("nodes", None),
            P("nodes", None),
            P("nodes", None),
            P("nodes"),
            P(),
            P(None, "feat"),
            P(None, "feat"),
            P("nodes", "feat"),
        ),
        out_specs=(P("nodes", "feat"), P("nodes", "feat"), P("nodes", "feat")),
        check_vma=False,
    )
```

```python
import jax
import jax.numpy as jnp
from jax import lax
from jax.experimental import pallas as pl
from jax.experimental.pallas import tpu as pltpu
from jax.sharding import PartitionSpec as P

MESH = pl.DeviceIdType.MESH
ROWS = 4
RING = 8
FEAT = 8
BLKS = 8
BS = 128
WIDTH = 128
GROUP = 4
F32 = jnp.float32
BF16 = jnp.bfloat16
VMEM = pl.BlockSpec(memory_space=pltpu.VMEM)
SMEM = pl.BlockSpec(memory_space=pltpu.SMEM)
DMA = pltpu.SemaphoreType.DMA


def whereabouts():
    node, feat = lax.axis_index("nodes"), lax.axis_index("feat")
    return lax.div(node, RING), lax.rem(node, RING), feat


def node_at(y, z, dy, dz):
    return lax.rem(y + dy + ROWS, ROWS) * RING + lax.rem(z + dz + RING, RING)


def feat_at(f, dx, dc):
    core = lax.rem(f, 2)
    chip = lax.div(f, 2)
    return lax.rem(chip + dx, 4) * 2 + lax.rem(core + dc, 2)


def greet(partners):
    barrier = pltpu.get_barrier_semaphore()
    for partner in partners:
        pl.semaphore_signal(barrier, inc=1, device_id=partner, device_id_type=MESH)
    pl.semaphore_wait(barrier, len(partners))


def send(src, dst, send_sem, recv_sem, device):
    return pltpu.make_async_remote_copy(
        src_ref=src,
        dst_ref=dst,
        send_sem=send_sem,
        recv_sem=recv_sem,
        device_id=device,
        device_id_type=MESH,
    )


FROM_BELOW = [(7, 0), (7, 1), (6, 0), (6, 1), (5, 0), (5, 1), (4, 0)]
FROM_ABOVE = [(1, 0), (1, 1), (2, 0), (2, 1), (3, 0), (3, 1), (4, 1)]


def gather_scratch():
    return [pltpu.VMEM((BLKS, BS, WIDTH), BF16)] * 7 + [
        pltpu.VMEM((RING, 3, 2, BS, WIDTH), BF16),
        DMA((2, 7)),
        DMA((2, 7)),
        DMA((RING, 3)),
        DMA((RING, 3)),
    ]


def gather_stages(place, field, table, ghost, scratch):
    y, z, f = place
    chunks = [field] + list(scratch[:7])
    picked, zs, zr, ys, yr = scratch[7:]
    above, below = (node_at(y, z, 0, 1), f), (node_at(y, z, 0, -1), f)

    def half(ref, h):
        return ref.at[pl.ds(4 * h, 4)]

    up, down = [], []
    for i in range(7):
        o, h = FROM_BELOW[i]
        up.append(
            send(half(chunks[(o + 1) % 8], h), half(chunks[o], h), zs.at[0, i], zr.at[0, i], above)
        )
        o, h = FROM_ABOVE[i]
        down.append(
            send(half(chunks[o - 1], h), half(chunks[o], h), zs.at[1, i], zr.at[1, i], below)
        )
    across = []

    def deal(o):
        zz = lax.rem(z + o, RING)
        base = (y * RING + zz) * 2
        chunk = chunks[o]
        for dy in (1, 3, 2):
            reader = lax.rem(y + dy, ROWS)
            for j in range(2):
                picked[o, dy - 1, j] = chunk[table[reader, zz, j]]
            copy = send(
                picked.at[o, dy - 1],
                ghost.at[pl.ds(base, 2)],
                ys.at[o, dy - 1],
                yr.at[o, dy - 1],
                (node_at(y, z, dy, 0), f),
            )
            copy.start()
            across.append(copy)
        for j in range(2):
            ghost[base + j] = chunk[table[y, zz, j]]

    for i in range(2):
        up[i].start()
        down[i].start()
    yield
    deal(0)
    yield
    for i in range(7):
        up[i].wait_recv()
        if i + 2 < 7:
            up[i + 2].start()
        down[i].wait_recv()
        if i + 2 < 6:
            down[i + 2].start()
        if i == 5:
            down[6].start()
        if i in (1, 3, 5):
            deal(FROM_BELOW[i][0])
            deal(FROM_ABOVE[i][0])
        if i == 6:
            deal(4)
        yield
    for copy in across:
        copy.wait()
    for copy in up + down:
        copy.wait_send()
    yield


def run(*stage_lists):
    live = list(stage_lists)
    while live:
        for stages in list(live):
            try:
                next(stages)
            except StopIteration:
                live.remove(stages)


def first_kernel(field, wants, weight_two, ghost, requests, two_rows, *scratch):
    place = y, z, f = whereabouts()
    table, ts, tr, ws, wr, local = scratch[:6]
    rest = scratch[6:]
    cols = [(node_at(y, z, dy, 0), f) for dy in (1, 2, 3)]
    ring = [(node_at(y, z, 0, 1), f), (node_at(y, z, 0, -1), f)]
    wide = [(lax.axis_index("nodes"), lax.rem(f + d, FEAT)) for d in range(1, FEAT)]
    greet(cols + ring + wide)
    asks = []
    for dy in (1, 2, 3):
        copy = send(
            wants.at[lax.rem(y + dy, ROWS)],
            requests.at[y],
            ts.at[dy - 1],
            tr.at[dy - 1],
            cols[dy - 1],
        )
        copy.start()
        asks.append(copy)
    stages = gather_stages(place, field, table, ghost, rest)
    next(stages)
    parts = []
    for d in range(1, FEAT):
        copy = send(
            weight_two.at[lax.rem(f + d, FEAT)],
            two_rows.at[f],
            ws.at[d - 1],
            wr.at[d - 1],
            wide[d - 1],
        )
        copy.start()
        parts.append(copy)
    two_rows[f] = weight_two[f]
    requests[y] = wants[y]
    for copy in asks:
        copy.wait_recv()
    move = pltpu.make_async_copy(requests, table, local)
    move.start()
    move.wait()
    run(stages)
    for copy in asks:
        copy.wait_send()
    for copy in parts:
        copy.wait()


def fetch_first(field, wants, weight_two):
    return pl.pallas_call(
        first_kernel,
        out_shape=(
            jax.ShapeDtypeStruct((2 * ROWS * RING, BS, WIDTH), BF16),
            jax.ShapeDtypeStruct((ROWS, RING, 128), jnp.int32),
            jax.ShapeDtypeStruct((FEAT, 128, WIDTH), BF16),
        ),
        in_specs=[VMEM] * 3,
        out_specs=(VMEM,) * 3,
        scratch_shapes=[
            pltpu.SMEM((ROWS, RING, 128), jnp.int32),
            DMA((3,)),
            DMA((3,)),
            DMA((7,)),
            DMA((7,)),
            DMA(()),
        ]
        + gather_scratch(),
        compiler_params=pltpu.CompilerParams(collective_id=0, has_side_effects=True),
    )(field, wants, weight_two)


def spread_rows(steps, slots, tiles, shares, field, ghost, table, out):
    @pl.loop(0, BLKS)
    def _(r):
        def advance(t, total):
            first = t * GROUP
            left = jnp.concatenate([table[tiles[r, first + g]] for g in range(GROUP)], axis=1)
            right = jnp.concatenate([ghost[slots[r, first + g]] for g in range(GROUP)], axis=0)
            return total + jnp.dot(left, right, preferred_element_type=F32)

        total = lax.fori_loop(0, steps[r], advance, jnp.zeros((BS, WIDTH), F32))
        out[r] = (field[r].astype(F32) + shares[r] * total).astype(out.dtype)


def share_rows(steps, slots, tiles, shares, field, turned, totals, out):
    @pl.loop(0, 64)
    def _(s):
        totals[s] = jnp.zeros((BS, WIDTH), F32)

    @pl.loop(0, BLKS)
    def _(r):
        block = field[r]

        def advance(t, carry):
            first = t * GROUP
            left = jnp.concatenate([turned[tiles[r, first + g]] for g in range(GROUP)], axis=0)
            terms = shares[r] * jnp.dot(left, block, preferred_element_type=F32)
            for g in range(GROUP):
                totals[slots[r, first + g]] += terms[g * BS : (g + 1) * BS]
            return carry

        lax.fori_loop(0, steps[r], advance, 0)

    @pl.loop(0, 64)
    def _(s):
        out[s] = totals[s].astype(BF16)


def local_kernel(steps, slots, tiles, shares, field, ghost, cot, table, out, partial, turned, totals):
    @pl.loop(0, 17)
    def _(t):
        turned[t] = table[t].T

    share_rows(steps, slots, tiles, shares, cot, turned, totals, partial)
    spread_rows(steps, slots, tiles, shares, field, ghost, table, out)


def spread_both(plan, field, ghost, cot, table):
    return pl.pallas_call(
        local_kernel,
        out_shape=(
            jax.ShapeDtypeStruct((BLKS, BS, WIDTH), BF16),
            jax.ShapeDtypeStruct((64, BS, WIDTH), BF16),
        ),
        in_specs=[SMEM] * 4 + [VMEM] * 4,
        out_specs=(VMEM,) * 2,
        scratch_shapes=[
            pltpu.VMEM((17, BS, BS), BF16),
            pltpu.VMEM((64, BS, WIDTH), F32),
        ],
    )(*plan, field, ghost, cot, table)


def spread_one(plan, field, ghost, table):
    return pl.pallas_call(
        spread_rows,
        out_shape=jax.ShapeDtypeStruct((BLKS, BS, WIDTH), BF16),
        in_specs=[SMEM] * 4 + [VMEM] * 3,
        out_specs=VMEM,
    )(*plan, field, ghost, table)


def widen_scratch():
    return [DMA((4,)), DMA((4,)), DMA((4,)), DMA((4,))]


def widen_stages(place, own, wide, scratch):
    y, z, f = place
    node = lax.axis_index("nodes")
    xs, xr, cs, cr = scratch
    twin = (node, feat_at(f, 0, 1))
    far = []
    for i, dx in enumerate((1, 3, 2)):
        copy = send(own, wide.at[f], xs.at[i], xr.at[i], (node, feat_at(f, dx, 0)))
        copy.start()
        far.append(copy)
    near = []
    for i, dx in enumerate((0, 3, 1, 2)):
        source = feat_at(f, dx, 0)
        if i > 0:
            far[i - 1].wait_recv()
        block = wide.at[source] if i > 0 else own
        copy = send(block, wide.at[source], cs.at[i], cr.at[i], twin)
        copy.start()
        near.append(copy)
        yield
    for copy in near:
        copy.wait_recv()
    for copy in near + far:
        copy.wait_send()
    yield


def widen_partners(place):
    node = lax.axis_index("nodes")
    f = place[2]
    return [(node, feat_at(f, dx, 0)) for dx in (1, 2, 3)] + [(node, feat_at(f, 0, 1))]


TO_ABOVE = [(4, 0), (3, 0), (3, 1), (2, 0), (2, 1), (1, 0), (1, 1)]
TO_BELOW = [(4, 1), (5, 1), (5, 0), (6, 1), (6, 0), (7, 1), (7, 0)]


def settle_scratch():
    return [
        pltpu.VMEM((RING, 3, 2, BS, WIDTH), BF16),
        pltpu.VMEM((RING, BLKS, BS, WIDTH), BF16),
        pltpu.VMEM((2, 7, 4, BS, WIDTH), BF16),
        DMA((RING, 3)),
        DMA((RING, 3)),
        DMA((2, 7)),
        DMA((2, 7)),
    ]


def settle_stages(place, partial, table, own, out, scratch):
    y, z, f = place
    landed, held, came, ys, yr, zs, zr = scratch
    above, below = (node_at(y, z, 0, 1), f), (node_at(y, z, 0, -1), f)
    order = (4, 3, 5, 2, 6, 1, 7, 0)
    across = {}
    for o in order:
        zz = lax.rem(z + o, RING)
        for dy in (1, 3, 2):
            owner = lax.rem(y + dy, ROWS)
            copy = send(
                partial.at[pl.ds((owner * RING + zz) * 2, 2)],
                landed.at[o, dy - 1],
                ys.at[o, dy - 1],
                yr.at[o, dy - 1],
                (node_at(y, z, dy, 0), f),
            )
            copy.start()
            across[o, dy] = copy
    yield

    def gathered(o, h, extras, base, store):
        zz = lax.rem(z + o, RING)
        sources, where = [], []
        for dy in range(ROWS):
            reader = lax.rem(y + ROWS - dy, ROWS)
            for j in range(2):
                where.append(table[reader, zz, j])
                sources.append((dy, j))
        marks = [
            [jnp.where(where[i] == 4 * h + b, 1.0, 0.0).astype(F32) for i in range(8)]
            for b in range(4)
        ]
        first = (y * RING + zz) * 2

        @pl.loop(0, BS // 16)
        def _(t):
            rows = pl.ds(pl.multiple_of(t * 16, 16), 16)
            values = []
            for dy, j in sources:
                if dy == 0:
                    value = partial[first + j, rows, :]
                else:
                    value = landed[o, dy - 1, j, rows, :]
                values.append(value.astype(F32))
            for b in range(4):
                total = marks[b][0] * values[0]
                for i in range(1, 8):
                    total = total + marks[b][i] * values[i]
                for lane, index in extras:
                    total = total + came[lane, index, b, rows, :].astype(F32)
                if base is not None:
                    total = total + base[4 * h + b, rows, :].astype(F32)
                store[4 * h + b, rows, :] = total.astype(BF16)

    def piece(lane, index, o, h):
        return send(
            held.at[o, pl.ds(4 * h, 4)],
            came.at[lane, index],
            zs.at[lane, index],
            zr.at[lane, index],
            above if lane == 0 else below,
        )

    def feeds(lane, o, h):
        lists = (TO_ABOVE, TO_BELOW)
        step = 1 if lane == 0 else -1
        source = (o + step) % 8
        return [(lane, i) for i, item in enumerate(lists[lane]) if item == (source, h)]

    pieces = {}

    def land(o):
        for dy in (1, 2, 3):
            across[o, dy].wait_recv()

    def forward(lane, index):
        o, h = (TO_ABOVE, TO_BELOW)[lane][index]
        extras = feeds(lane, o, h)
        for key in extras:
            pieces[key].wait_recv()
        gathered(o, h, extras, None, held.at[o])
        pieces[lane, index] = piece(lane, index, o, h)
        pieces[lane, index].start()

    land(4)
    forward(0, 0)
    forward(1, 0)
    yield
    for step, (a, b) in enumerate(((3, 5), (2, 6), (1, 7))):
        land(a)
        land(b)
        for half in range(2):
            forward(0, 1 + 2 * step + half)
            forward(1, 1 + 2 * step + half)
            yield
    land(0)
    for half in range(2):
        extras = feeds(0, 0, half) + feeds(1, 0, half)
        for key in extras:
            pieces[key].wait_recv()
        gathered(0, half, extras, own, out)
        yield
    for copy in list(across.values()) + list(pieces.values()):
        copy.wait_send()
    yield


def column(y, z, f):
    return [(node_at(y, z, dy, 0), f) for dy in (1, 2, 3)]


def times(wide, weight, rows):
    total = None
    for pair in range(FEAT // 2):
        left = jnp.concatenate([wide[2 * pair, rows, :], wide[2 * pair + 1, rows, :]], axis=1)
        right = jnp.concatenate([weight[2 * pair], weight[2 * pair + 1]], axis=0)
        term = jnp.dot(left, right, preferred_element_type=F32)
        total = term if total is None else total + term
    return total


TILE = 256


def second_kernel(
    table,
    agg,
    partial,
    cot,
    weight_one,
    weight_two,
    agg_wide,
    hidden_wide,
    pre_one,
    mixed,
    back,
    *scratch,
):
    place = y, z, f = whereabouts()
    ring = [(node_at(y, z, 0, 1), f), (node_at(y, z, 0, -1), f)]
    greet(column(y, z, f) + ring + widen_partners(place))
    agg_wide[f] = agg[...]
    first = widen_stages(place, agg, agg_wide, scratch[:4])
    settle = settle_stages(place, partial, table, cot, back, scratch[8:])
    next(first)
    next(settle)
    next(first)
    next(settle)
    next(first)
    next(settle)
    run(first)

    @pl.loop(0, 1024 // TILE)
    def _(t):
        rows = pl.ds(pl.multiple_of(t * TILE, TILE), TILE)
        pre = times(agg_wide, weight_one, rows)
        pre_one[rows, :] = pre
        hidden_wide[f, rows, :] = (pre * jax.nn.sigmoid(pre)).astype(BF16)

    second = widen_stages(place, hidden_wide.at[f], hidden_wide, scratch[4:8])
    next(second)
    next(settle)
    next(settle)
    next(second)
    next(settle)
    next(second)
    next(settle)
    run(second)

    @pl.loop(0, 1024 // TILE)
    def _(t):
        rows = pl.ds(pl.multiple_of(t * TILE, TILE), TILE)
        mixed[rows, :] = times(hidden_wide, weight_two, rows).astype(BF16)

    run(settle)


def middle(table, agg, partial, cot, weight_one, weight_two):
    wide = jax.ShapeDtypeStruct((FEAT, 1024, WIDTH), BF16)
    return pl.pallas_call(
        second_kernel,
        out_shape=(
            wide,
            wide,
            jax.ShapeDtypeStruct((1024, WIDTH), F32),
            jax.ShapeDtypeStruct((1024, WIDTH), BF16),
            jax.ShapeDtypeStruct((BLKS, BS, WIDTH), BF16),
        ),
        in_specs=[SMEM] + [VMEM] * 5,
        out_specs=(VMEM,) * 5,
        scratch_shapes=widen_scratch() + widen_scratch() + settle_scratch(),
        compiler_params=pltpu.CompilerParams(collective_id=1, has_side_effects=True),
    )(table, agg, partial, cot, weight_one, weight_two)


def reduce_scratch():
    return [
        pltpu.VMEM((ROWS, 256, WIDTH), F32),
        pltpu.VMEM((3, 256, WIDTH), F32),
        pltpu.VMEM((RING, 32, WIDTH), F32),
        pltpu.VMEM((7, 32, WIDTH), F32),
        DMA((3,)),
        DMA((3,)),
        DMA((7,)),
        DMA((7,)),
    ]


def reduce_stages(place, out, scratch):
    y, z, f = place
    shares, came, mine, landed, ys, yr, zs, zr = scratch
    across = []
    for dy in (1, 3, 2):
        copy = send(
            shares.at[lax.rem(y + dy, ROWS)],
            came.at[dy - 1],
            ys.at[dy - 1],
            yr.at[dy - 1],
            (node_at(y, z, dy, 0), f),
        )
        copy.start()
        across.append(copy)
    yield
    for copy in across:
        copy.wait_recv()
    for o in range(RING):
        rows = pl.ds(o * 32, 32)
        mine[o] = shares[y, rows, :] + came[0, rows, :] + came[1, rows, :] + came[2, rows, :]
    along = []
    for dz in (4, 3, 5, 2, 6, 1, 7):
        copy = send(
            mine.at[lax.rem(z + dz, RING)],
            landed.at[dz - 1],
            zs.at[dz - 1],
            zr.at[dz - 1],
            (node_at(y, z, 0, dz), f),
        )
        copy.start()
        along.append(copy)
    yield
    for copy in along:
        copy.wait_recv()
    total = mine[z]
    for i in range(7):
        total = total + landed[i]
    out[...] = total
    for copy in across + along:
        copy.wait_send()
    yield


def outer(wide, right, shares):
    @pl.loop(0, ROWS)
    def _(i):
        for j in range(2):
            shares[i, pl.ds(j * 128, 128), :] = lax.dot_general(
                wide[2 * i + j], right[...], (((0,), (0,)), ((), ())), preferred_element_type=F32
            )


def third_kernel(
    table,
    mixed,
    back,
    agg_wide,
    hidden_wide,
    pre_one,
    two_rows,
    ghost,
    grad_one,
    grad_two,
    back_wide,
    back_pre,
    back_flat,
    *scratch,
):
    place = y, z, f = whereabouts()
    along = [(node_at(y, z, 0, dz), f) for dz in range(1, RING)]
    greet(column(y, z, f) + along + widen_partners(place))
    gather = gather_stages(place, mixed, table, ghost, scratch[:12])
    next(gather)
    back_wide[f] = back[...].reshape(1024, WIDTH)
    widen = widen_stages(place, back_wide.at[f], back_wide, scratch[12:16])
    next(widen)
    next(gather)
    back_flat[...] = back[...].reshape(1024, WIDTH)
    next(widen)
    outer(hidden_wide, back_flat, scratch[24])
    next(gather)
    next(gather)
    two = reduce_stages(place, grad_two, scratch[24:32])
    next(two)
    next(widen)
    next(gather)
    next(widen)
    next(gather)
    run(widen)

    @pl.loop(0, 1024 // TILE)
    def _(t):
        rows = pl.ds(pl.multiple_of(t * TILE, TILE), TILE)
        total = None
        for pair in range(FEAT // 2):
            left = jnp.concatenate(
                [back_wide[2 * pair, rows, :], back_wide[2 * pair + 1, rows, :]], axis=1
            )
            right = jnp.concatenate([two_rows[2 * pair], two_rows[2 * pair + 1]], axis=1)
            term = lax.dot_general(
                left, right, (((1,), (1,)), ((), ())), preferred_element_type=F32
            )
            total = term if total is None else total + term
        pre = pre_one[rows, :]
        sigma = jax.nn.sigmoid(pre)
        back_pre[rows, :] = (total * sigma * (1.0 + pre * (1.0 - sigma))).astype(BF16)

    next(gather)
    outer(agg_wide, back_pre, scratch[16])
    one = reduce_stages(place, grad_one, scratch[16:24])
    next(one)
    next(gather)
    next(two)
    next(gather)
    next(one)
    run(gather, two, one)


def last(table, mixed, back, agg_wide, hidden_wide, pre_one, two_rows):
    return pl.pallas_call(
        third_kernel,
        out_shape=(
            jax.ShapeDtypeStruct((2 * ROWS * RING, BS, WIDTH), BF16),
            jax.ShapeDtypeStruct((32, WIDTH), F32),
            jax.ShapeDtypeStruct((32, WIDTH), F32),
        ),
        in_specs=[SMEM] + [VMEM] * 6,
        out_specs=(VMEM,) * 3,
        scratch_shapes=[
            pltpu.VMEM((FEAT, 1024, WIDTH), BF16),
            pltpu.VMEM((1024, WIDTH), BF16),
            pltpu.VMEM((1024, WIDTH), BF16),
        ]
        + gather_scratch()
        + widen_scratch()
        + reduce_scratch()
        + reduce_scratch(),
        compiler_params=pltpu.CompilerParams(collective_id=2, has_side_effects=True),
    )(table, mixed, back, agg_wide, hidden_wide, pre_one, two_rows)


def on_device(
    features, ghosts, slots, tile_ids, degrees, tile_table, weight_one, weight_two, cotangent
):
    blocks = features.reshape(BLKS, BS, WIDTH)
    cot = cotangent.reshape(BLKS, BS, WIDTH)
    wants = jnp.pad(ghosts.reshape(ROWS, RING, 2), ((0, 0), (0, 0), (0, 126)))
    position = lax.broadcasted_iota(jnp.int32, slots.shape, 1)
    live_tiles = jnp.where(position < degrees[:, None], tile_ids, 16)
    steps = (degrees + GROUP - 1) // GROUP
    plan = (steps, slots, live_tiles, lax.rsqrt(degrees.astype(F32)))
    table = jnp.pad(tile_table, ((0, 1), (0, 0), (0, 0)))
    one = weight_one.reshape(FEAT, 128, WIDTH)
    two = weight_two.reshape(FEAT, 128, WIDTH)
    ghost, requests, two_rows = fetch_first(blocks, wants, two)
    agg, partial = spread_both(plan, blocks, ghost, cot, table)
    agg_wide, hidden_wide, pre_one, mixed, back = middle(
        requests, agg.reshape(1024, WIDTH), partial, cot, one, two
    )
    mixed = mixed.reshape(BLKS, BS, WIDTH)
    ghost_two, grad_one, grad_two = last(
        requests, mixed, back, agg_wide, hidden_wide, pre_one, two_rows
    )
    output = spread_one(plan, mixed, ghost_two, table)
    return (output.reshape(1024, WIDTH), grad_one, grad_two)


def solution(mesh):
    return jax.shard_map(
        on_device,
        mesh=mesh,
        in_specs=(
            P("nodes", "feat"),
            P("nodes", None),
            P("nodes", None),
            P("nodes", None),
            P("nodes"),
            P(),
            P(None, "feat"),
            P(None, "feat"),
            P("nodes", "feat"),
        ),
        out_specs=(P("nodes", "feat"), P("nodes", "feat"), P("nodes", "feat")),
        check_vma=False,
    )
```

```python
import jax
import jax.numpy as jnp
from jax import lax
from jax.experimental import pallas as pl
from jax.experimental.pallas import tpu as pltpu
from jax.sharding import PartitionSpec as P

MESH = pl.DeviceIdType.MESH
ROWS = 4
RING = 8
FEAT = 8
BLKS = 8
BS = 128
WIDTH = 128
GROUP = 4
DEPTH = 24
PART = 256
PARTS = 4
F32 = jnp.float32
BF16 = jnp.bfloat16
VMEM = pl.BlockSpec(memory_space=pltpu.VMEM)
SMEM = pl.BlockSpec(memory_space=pltpu.SMEM)
DMA = pltpu.SemaphoreType.DMA


def whereabouts():
    node, feat = lax.axis_index("nodes"), lax.axis_index("feat")
    return lax.div(node, RING), lax.rem(node, RING), feat


def node_at(y, z, dy, dz):
    return lax.rem(y + dy + ROWS, ROWS) * RING + lax.rem(z + dz + RING, RING)


def feat_at(f, dx, dc):
    core = lax.rem(f, 2)
    chip = lax.div(f, 2)
    return lax.rem(chip + dx, 4) * 2 + lax.rem(core + dc, 2)


def greet(partners):
    barrier = pltpu.get_barrier_semaphore()
    for partner in partners:
        pl.semaphore_signal(barrier, inc=1, device_id=partner, device_id_type=MESH)
    pl.semaphore_wait(barrier, len(partners))


def send(src, dst, send_sem, recv_sem, device):
    return pltpu.make_async_remote_copy(
        src_ref=src,
        dst_ref=dst,
        send_sem=send_sem,
        recv_sem=recv_sem,
        device_id=device,
        device_id_type=MESH,
    )


def wanted(table, y, reader, j, zz):
    return table[reader, j, y * RING + zz]


FROM_BELOW = [(7, 0), (7, 1), (6, 0), (6, 1), (5, 0), (5, 1), (4, 0)]
FROM_ABOVE = [(1, 0), (1, 1), (2, 0), (2, 1), (3, 0), (3, 1), (4, 1)]


def gather_scratch():
    return [pltpu.VMEM((BLKS, BS, WIDTH), BF16)] * 7 + [
        pltpu.VMEM((RING, 3, 2, BS, WIDTH), BF16),
        pltpu.VMEM((2 * ROWS * RING, BS, WIDTH), BF16),
        DMA((2, 7)),
        DMA((2, 7)),
        DMA((RING, 3)),
        DMA((RING, 3)),
    ]


def gather_stages(place, field, table, scratch):
    y, z, f = place
    chunks = [field] + list(scratch[:7])
    picked, ghost, zs, zr, ys, yr = scratch[7:]
    above, below = (node_at(y, z, 0, 1), f), (node_at(y, z, 0, -1), f)

    def half(ref, h):
        return ref.at[pl.ds(4 * h, 4)]

    up, down = [], []
    for i in range(7):
        o, h = FROM_BELOW[i]
        up.append(
            send(half(chunks[(o + 1) % 8], h), half(chunks[o], h), zs.at[0, i], zr.at[0, i], above)
        )
        o, h = FROM_ABOVE[i]
        down.append(
            send(half(chunks[o - 1], h), half(chunks[o], h), zs.at[1, i], zr.at[1, i], below)
        )
    across = []

    def deal(o):
        zz = lax.rem(z + o, RING)
        base = (y * RING + zz) * 2
        chunk = chunks[o]
        for dy in (1, 3, 2):
            reader = lax.rem(y + dy, ROWS)
            for j in range(2):
                picked[o, dy - 1, j] = chunk[wanted(table, y, reader, j, zz)]
            copy = send(
                picked.at[o, dy - 1],
                ghost.at[pl.ds(base, 2)],
                ys.at[o, dy - 1],
                yr.at[o, dy - 1],
                (node_at(y, z, dy, 0), f),
            )
            copy.start()
            across.append(copy)
        for j in range(2):
            ghost[base + j] = chunk[wanted(table, y, y, j, zz)]

    for i in range(2):
        up[i].start()
        down[i].start()
        yield
    deal(0)
    yield
    for i in range(7):
        up[i].wait_recv()
        if i + 2 < 7:
            up[i + 2].start()
        down[i].wait_recv()
        if i + 2 < 6:
            down[i + 2].start()
        if i == 5:
            down[6].start()
        if i in (1, 3, 5):
            deal(FROM_BELOW[i][0])
            deal(FROM_ABOVE[i][0])
        if i == 6:
            deal(4)
        yield
    for copy in across:
        copy.wait()
    for copy in up + down:
        copy.wait_send()
    yield


def step(*stage_lists):
    for stages in stage_lists:
        next(stages, None)


def drain(stages):
    for _ in stages:
        pass


def share_kernel(degrees, slots, tiles, cot, table, out, turned, totals):
    for t in range(16):
        turned[t] = table[t].T
    turned[16] = jnp.zeros((BS, BS), BF16)

    @pl.loop(0, 64)
    def _(s):
        totals[s] = jnp.zeros((BS, WIDTH), F32)

    @pl.loop(0, BLKS)
    def _(r):
        block = cot[r]
        degree = degrees[r]
        share = lax.rsqrt(jnp.full((1, WIDTH), degree.astype(F32)))

        def advance(t, carry):
            first = t * GROUP
            picks = [
                turned[jnp.where(first + g < degree, tiles[r, first + g], 16)] for g in range(GROUP)
            ]
            terms = share * jnp.dot(
                jnp.concatenate(picks, axis=0), block, preferred_element_type=F32
            )
            for g in range(GROUP):
                totals[slots[r, first + g]] += terms[g * BS : (g + 1) * BS]
            return carry

        lax.fori_loop(0, lax.div(degree + GROUP - 1, GROUP), advance, 0)

    @pl.loop(0, 64)
    def _(s):
        out[s] = totals[s].astype(BF16)


def share_out(degrees, slots, tiles, cot, table):
    return pl.pallas_call(
        share_kernel,
        out_shape=jax.ShapeDtypeStruct((64, BS, WIDTH), BF16),
        in_specs=[SMEM] * 3 + [VMEM] * 2,
        out_specs=VMEM,
        scratch_shapes=[
            pltpu.VMEM((17, BS, BS), BF16),
            pltpu.VMEM((64, BS, WIDTH), F32),
        ],
    )(degrees, slots, tiles, cot, table)


def spread_rows(first, last, degrees, slots, tiles, field, ghost, table, put):
    @pl.loop(first, last)
    def _(r):
        degree = degrees[r]
        share = lax.rsqrt(jnp.full((1, WIDTH), degree.astype(F32)))
        total = jnp.zeros((BS, WIDTH), F32)
        for t in range(DEPTH // GROUP):
            entries = range(t * GROUP, (t + 1) * GROUP)
            left = jnp.concatenate(
                [table[jnp.where(k < degree, tiles[r, k], 16)] for k in entries], axis=1
            )
            right = jnp.concatenate([ghost[slots[r, k]] for k in entries], axis=0)
            total = total + jnp.dot(left, right, preferred_element_type=F32)
        put(r, (field[r].astype(F32) + share * total).astype(BF16))


def widen_scratch():
    return [DMA((PARTS, 3)), DMA((PARTS, 3)), DMA((PARTS, 4)), DMA((PARTS, 4))]


class Widen:
    def __init__(self, place, wide, scratch):
        self.f = place[2]
        self.node = lax.axis_index("nodes")
        self.wide = wide
        self.sems = scratch
        self.far, self.near = {}, {}

    def piece(self, owner, q):
        return self.wide.at[owner, pl.ds(q * PART, PART)]

    def push(self, q):
        xs, xr = self.sems[:2]
        mine = self.piece(self.f, q)
        for i, dx in enumerate((1, 3, 2)):
            copy = send(
                mine, mine, xs.at[q, i], xr.at[q, i], (self.node, feat_at(self.f, dx, 0))
            )
            copy.start()
            self.far[q, i] = copy
        self.pass_on(q, 3, self.f)

    def pass_on(self, q, i, owner):
        cs, cr = self.sems[2:]
        block = self.piece(owner, q)
        copy = send(
            block, block, cs.at[q, i], cr.at[q, i], (self.node, feat_at(self.f, 0, 1))
        )
        copy.start()
        self.near[q, i] = copy

    def relay(self, q):
        for i, dx in enumerate((3, 1, 2)):
            self.far[q, i].wait_recv()
            self.pass_on(q, i, feat_at(self.f, dx, 0))

    def ready(self, q):
        for i in range(4):
            self.near[q, i].wait_recv()

    def finish(self):
        for copy in list(self.far.values()) + list(self.near.values()):
            copy.wait_send()


TO_ABOVE = [(4, 0), (3, 0), (3, 1), (2, 0), (2, 1), (1, 0), (1, 1)]
TO_BELOW = [(4, 1), (5, 1), (5, 0), (6, 1), (6, 0), (7, 1), (7, 0)]


def settle_scratch():
    return [
        pltpu.VMEM((RING, 3, 2, BS, WIDTH), BF16),
        pltpu.VMEM((RING, BLKS, BS, WIDTH), BF16),
        pltpu.VMEM((2, 7, 4, BS, WIDTH), BF16),
        DMA((RING, 3)),
        DMA((RING, 3)),
        DMA((2, 7)),
        DMA((2, 7)),
    ]


def settle_stages(place, partial, table, own, wide, scratch):
    y, z, f = place
    landed, held, came, ys, yr, zs, zr = scratch
    above, below = (node_at(y, z, 0, 1), f), (node_at(y, z, 0, -1), f)
    across = {}
    for o in (4, 3, 5, 2, 6, 1, 7, 0):
        zz = lax.rem(z + o, RING)
        for dy in (1, 3, 2):
            owner = lax.rem(y + dy, ROWS)
            copy = send(
                partial.at[pl.ds((owner * RING + zz) * 2, 2)],
                landed.at[o, dy - 1],
                ys.at[o, dy - 1],
                yr.at[o, dy - 1],
                (node_at(y, z, dy, 0), f),
            )
            copy.start()
            across[o, dy] = copy
    yield

    def gathered(o, h, extras):
        zz = lax.rem(z + o, RING)
        sources, where = [], []
        for dy in range(ROWS):
            reader = lax.rem(y + ROWS - dy, ROWS)
            for j in range(2):
                where.append(wanted(table, y, reader, j, zz))
                sources.append((dy, j))
        marks = [
            [jnp.where(where[i] == 4 * h + b, 1.0, 0.0).astype(F32) for i in range(8)]
            for b in range(4)
        ]
        first = (y * RING + zz) * 2

        @pl.loop(0, BS // 16)
        def _(t):
            rows = pl.ds(pl.multiple_of(t * 16, 16), 16)
            values = []
            for dy, j in sources:
                if dy == 0:
                    value = partial[first + j, rows, :]
                else:
                    value = landed[o, dy - 1, j, rows, :]
                values.append(value.astype(F32))
            for b in range(4):
                block = 4 * h + b
                total = marks[b][0] * values[0]
                for i in range(1, 8):
                    total = total + marks[b][i] * values[i]
                for lane, index in extras:
                    total = total + came[lane, index, b, rows, :].astype(F32)
                if o == 0:
                    total = total + own[block, rows, :].astype(F32)
                    flat = pl.ds(pl.multiple_of(block * BS + t * 16, 16), 16)
                    wide[f, flat, :] = total.astype(BF16)
                else:
                    held[o, block, rows, :] = total.astype(BF16)

    def piece(lane, index, o, h):
        return send(
            held.at[o, pl.ds(4 * h, 4)],
            came.at[lane, index],
            zs.at[lane, index],
            zr.at[lane, index],
            above if lane == 0 else below,
        )

    def feeds(lane, o, h):
        lists = (TO_ABOVE, TO_BELOW)
        source = (o + (1 if lane == 0 else -1)) % 8
        return [(lane, i) for i, item in enumerate(lists[lane]) if item == (source, h)]

    pieces = {}

    def land(o):
        for dy in (1, 2, 3):
            across[o, dy].wait_recv()

    def forward(lane, index):
        o, h = (TO_ABOVE, TO_BELOW)[lane][index]
        extras = feeds(lane, o, h)
        for key in extras:
            pieces[key].wait_recv()
        gathered(o, h, extras)
        pieces[lane, index] = piece(lane, index, o, h)
        pieces[lane, index].start()

    land(4)
    forward(0, 0)
    forward(1, 0)
    yield
    for turn, (a, b) in enumerate(((3, 5), (2, 6), (1, 7))):
        land(a)
        land(b)
        for half in range(2):
            forward(0, 1 + 2 * turn + half)
            forward(1, 1 + 2 * turn + half)
            yield
    land(0)
    for half in range(2):
        extras = feeds(0, 0, half) + feeds(1, 0, half)
        for key in extras:
            pieces[key].wait_recv()
        gathered(0, half, extras)
        yield
    for copy in list(across.values()) + list(pieces.values()):
        copy.wait_send()
    yield


def times(wide, weight, rows):
    total = None
    for pair in range(FEAT // 2):
        left = jnp.concatenate([wide[2 * pair, rows, :], wide[2 * pair + 1, rows, :]], axis=1)
        right = jnp.concatenate([weight[2 * pair], weight[2 * pair + 1]], axis=0)
        term = jnp.dot(left, right, preferred_element_type=F32)
        total = term if total is None else total + term
    return total


def times_turned(wide, weight, rows):
    total = None
    for pair in range(FEAT // 2):
        left = jnp.concatenate([wide[2 * pair, rows, :], wide[2 * pair + 1, rows, :]], axis=1)
        right = jnp.concatenate([weight[2 * pair], weight[2 * pair + 1]], axis=1)
        term = lax.dot_general(left, right, (((1,), (1,)), ((), ())), preferred_element_type=F32)
        total = term if total is None else total + term
    return total


def reduce_scratch():
    return [
        pltpu.VMEM((ROWS, 256, WIDTH), BF16),
        pltpu.VMEM((3, 256, WIDTH), BF16),
        pltpu.VMEM((RING, 32, WIDTH), F32),
        pltpu.VMEM((7, 32, WIDTH), F32),
        DMA((3,)),
        DMA((3,)),
        DMA((7,)),
        DMA((7,)),
    ]


def reduce_stages(place, wide, right, out, scratch):
    y, z, f = place
    shares, came, mine, landed, ys, yr, zs, zr = scratch
    across = []

    def fill(owner):
        for j in range(2):
            value = lax.dot_general(
                wide[2 * owner + j],
                right(),
                (((0,), (0,)), ((), ())),
                preferred_element_type=F32,
            )
            shares[owner, pl.ds(j * 128, 128), :] = value.astype(BF16)

    for dy in (2, 1, 3):
        owner = lax.rem(y + dy, ROWS)
        fill(owner)
        copy = send(
            shares.at[owner],
            came.at[dy - 1],
            ys.at[dy - 1],
            yr.at[dy - 1],
            (node_at(y, z, dy, 0), f),
        )
        copy.start()
        across.append(copy)
    fill(y)
    yield
    for copy in across:
        copy.wait_recv()
    for o in range(RING):
        rows = pl.ds(o * 32, 32)
        total = shares[y, rows, :].astype(F32)
        for i in range(3):
            total = total + came[i, rows, :].astype(F32)
        mine[o] = total
    along = []
    for dz in (4, 3, 5, 2, 6, 1, 7):
        copy = send(
            mine.at[lax.rem(z + dz, RING)],
            landed.at[dz - 1],
            zs.at[dz - 1],
            zr.at[dz - 1],
            (node_at(y, z, 0, dz), f),
        )
        copy.start()
        along.append(copy)
    yield
    for copy in along:
        copy.wait_recv()
    total = mine[z]
    for i in range(7):
        total = total + landed[i]
    out[...] = total
    for copy in across + along:
        copy.wait_send()
    yield


SIZES = (13, 13, 4, 4, 4, 7, 8, 8)


def whole_scratch():
    return (
        gather_scratch()
        + gather_scratch()
        + widen_scratch()
        + widen_scratch()
        + widen_scratch()
        + settle_scratch()
        + reduce_scratch()
        + reduce_scratch()
    )


def whole_kernel(
    degrees,
    slots,
    tile_ids,
    wants,
    field,
    cot,
    partial,
    tile_table,
    weight_one,
    weight_two,
    out,
    grad_one,
    grad_two,
    requests,
    table,
    tiles,
    two_rows,
    agg_wide,
    hidden_wide,
    back_wide,
    pre_one,
    mixed,
    back_pre,
    ts,
    tr,
    ws,
    wr,
    local,
    *scratch,
):
    place = y, z, f = whereabouts()
    node = lax.axis_index("nodes")
    cuts = [sum(SIZES[:i]) for i in range(len(SIZES) + 1)]
    groups = [scratch[cuts[i] : cuts[i + 1]] for i in range(len(SIZES))]
    column = [(node_at(y, z, dy, 0), f) for dy in (1, 2, 3)]
    along = [(node_at(y, z, 0, dz), f) for dz in range(1, RING)]
    feats = [(node, lax.rem(f + d, FEAT)) for d in range(1, FEAT)]
    greet(column + along + feats)

    asks = []
    for dy in (1, 2, 3):
        copy = send(wants, requests.at[y], ts.at[dy - 1], tr.at[dy - 1], column[dy - 1])
        copy.start()
        asks.append(copy)
    gather = gather_stages(place, field, table, groups[0])
    step(gather, gather)
    parts = []
    for d in range(1, FEAT):
        copy = send(
            weight_two.at[lax.rem(f + d, FEAT)],
            two_rows.at[f],
            ws.at[d - 1],
            wr.at[d - 1],
            feats[d - 1],
        )
        copy.start()
        parts.append(copy)
    two_rows[f] = weight_two[f]
    requests[y] = wants[...]
    for t in range(16):
        tiles[t] = tile_table[t]
    tiles[16] = jnp.zeros((BS, BS), BF16)
    for copy in asks:
        copy.wait_recv()
    move = pltpu.make_async_copy(requests, table, local)
    move.start()
    move.wait()
    for _ in range(8):
        step(gather)
    settle = settle_stages(place, partial, table, cot, back_wide, groups[5])
    step(settle)
    drain(gather)

    agg = Widen(place, agg_wide, groups[2])
    hid = Widen(place, hidden_wide, groups[3])
    for q in range(PARTS):

        def put(r, value):
            agg_wide[f, pl.ds(pl.multiple_of(r * BS, BS), BS), :] = value

        spread_rows(
            2 * q, 2 * q + 2, degrees, slots, tile_ids, field, groups[0][8], tiles, put
        )
        agg.push(q)

    def project(q):
        agg.ready(q)
        rows = pl.ds(q * PART, PART)
        pre = times(agg_wide, weight_one, rows)
        pre_one[rows, :] = pre
        hidden_wide[f, rows, :] = (pre * jax.nn.sigmoid(pre)).astype(BF16)
        hid.push(q)

    def mix(q):
        hid.ready(q)
        value = times(hidden_wide, weight_two, pl.ds(q * PART, PART)).astype(BF16)
        mixed[2 * q] = value[:BS]
        mixed[2 * q + 1] = value[BS:]

    agg.relay(0)
    step(settle)
    agg.relay(1)
    project(0)
    step(settle)
    agg.relay(2)
    project(1)
    step(settle)
    agg.relay(3)
    project(2)
    step(settle)
    project(3)
    hid.relay(0)
    step(settle)
    hid.relay(1)
    mix(0)
    step(settle)
    hid.relay(2)
    mix(1)
    second = gather_stages(place, mixed, table, groups[1])
    step(second)
    step(settle)
    hid.relay(3)
    mix(2)
    mix(3)
    step(second)

    back = Widen(place, back_wide, groups[4])
    step(settle)
    back.push(0)
    back.push(1)
    step(second)
    step(settle)
    back.push(2)
    back.push(3)
    step(second)

    two = reduce_stages(place, hidden_wide, lambda: back_wide[f], grad_two, groups[7])
    step(two)
    step(second)

    def backward(q):
        back.ready(q)
        rows = pl.ds(q * PART, PART)
        total = times_turned(back_wide, two_rows, rows)
        pre = pre_one[rows, :]
        sigma = jax.nn.sigmoid(pre)
        back_pre[rows, :] = (total * sigma * (1.0 + pre * (1.0 - sigma))).astype(BF16)

    for copy in parts:
        copy.wait()
    back.relay(0)
    back.relay(1)
    backward(0)
    step(second)
    back.relay(2)
    backward(1)
    step(second)
    back.relay(3)
    backward(2)
    backward(3)
    one = reduce_stages(place, agg_wide, lambda: back_pre[...], grad_one, groups[6])
    step(second)
    step(one)
    step(second)
    step(two)
    step(second)
    step(one)
    drain(second)

    def put_out(r, value):
        out[r] = value

    spread_rows(0, BLKS, degrees, slots, tile_ids, mixed, groups[1][8], tiles, put_out)
    drain(two)
    drain(one)
    drain(settle)
    for copy in asks:
        copy.wait_send()
    agg.finish()
    hid.finish()
    back.finish()


def whole(*operands):
    wide = pltpu.VMEM((FEAT, 1024, WIDTH), BF16)
    return pl.pallas_call(
        whole_kernel,
        out_shape=(
            jax.ShapeDtypeStruct((BLKS, BS, WIDTH), BF16),
            jax.ShapeDtypeStruct((32, WIDTH), F32),
            jax.ShapeDtypeStruct((32, WIDTH), F32),
        ),
        in_specs=[SMEM] * 3 + [VMEM] * 7,
        out_specs=(VMEM,) * 3,
        scratch_shapes=[
            pltpu.VMEM((ROWS, 2, 32), jnp.int32),
            pltpu.SMEM((ROWS, 2, 32), jnp.int32),
            pltpu.VMEM((17, BS, BS), BF16),
            pltpu.VMEM((FEAT, 128, WIDTH), BF16),
            wide,
            wide,
            wide,
            pltpu.VMEM((1024, WIDTH), F32),
            pltpu.VMEM((BLKS, BS, WIDTH), BF16),
            pltpu.VMEM((1024, WIDTH), BF16),
            DMA((3,)),
            DMA((3,)),
            DMA((7,)),
            DMA((7,)),
            DMA(()),
        ]
        + whole_scratch(),
        compiler_params=pltpu.CompilerParams(collective_id=0, has_side_effects=True),
    )(*operands)


def on_device(
    features, ghosts, slots, tile_ids, degrees, tile_table, weight_one, weight_two, cotangent
):
    blocks = features.reshape(BLKS, BS, WIDTH)
    cot = cotangent.reshape(BLKS, BS, WIDTH)
    one = weight_one.reshape(FEAT, 128, WIDTH)
    two = weight_two.reshape(FEAT, 128, WIDTH)
    partial = share_out(degrees, slots, tile_ids, cot, tile_table)
    output, grad_one, grad_two = whole(
        degrees, slots, tile_ids, ghosts.T, blocks, cot, partial, tile_table, one, two
    )
    return (output.reshape(1024, WIDTH), grad_one, grad_two)


def solution(mesh):
    return jax.shard_map(
        on_device,
        mesh=mesh,
        in_specs=(
            P("nodes", "feat"),
            P("nodes", None),
            P("nodes", None),
            P("nodes", None),
            P("nodes"),
            P(),
            P(None, "feat"),
            P(None, "feat"),
            P("nodes", "feat"),
        ),
        out_specs=(P("nodes", "feat"), P("nodes", "feat"), P("nodes", "feat")),
        check_vma=False,
    )
```
